32 devices in a mesh: lead: 2 (over x), tile: 16 (over z, y, core).
Axes of the slice: x: 2, y: 2, z: 4, core: 2. Of those that a mesh axis runs over, the one named last changes fastest.
Arguments:
- states: float32 [2, 2, 128, 128, 128], P('lead', None, None, 'tile'), may hold values from -6 to 6
- cotangents: float32 [2, 2, 128, 128, 128], P('lead', None, None, 'tile'), may hold values from -6 to 6
- w_conv: bfloat16 [1152, 512], replicated, may hold values from -0.1875 to 0.1875
- b_conv: float32 [512], replicated, may hold values from -3 to 3
- w_out: bfloat16 [512, 128], replicated, may hold values from -0.25 to 0.25
- forcing: float32 [365, 128], replicated, may hold values from -3 to 3
- land: int32 [128, 128], P('tile'), may hold values 0 or 1
- dates: int32 [2], replicated, may hold values from 0 to 364
Outputs:
- state_grads: float32 [2, 2, 128, 128, 128], P('lead', None, None, 'tile')
- w1_grad: float32 [1152, 512], P('tile')
- w2_grad: float32 [512, 128], P('tile')
- b1_grad: float32 [512], P('tile')
The draws below stay inside these ranges and needn't reach their ends.
Inputs may be any that keep to these rules, and one draw needn't show every extreme that they name: 1 marks an ocean column, 0 a land column.
All inputs are finite; a program needn't handle non-finite values. No bound on the sum of `land` on one device may be relied on, other than what follows from the above.
Results may differ from the reference program's by a relative error of at most 0.0056.
Values may be sent and summed in bfloat16 or wider, within the bound.
No kernel may reach another device: no remote copies, remote signals or barrier semaphores. Data moves between devices by JAX's collectives and lax.ppermute only.
A program may use at most 128 MiB of HBM per device.

```python
import math
import jax
import jax.numpy as jnp
from jax import lax

C = 128
H = 512
DAYS = 365
NX = 128
MB = 2
NY = 128
N_LEAD = 2


def place_ends(array, key, least, largest):
    index_at = [jax.random.randint(jax.random.fold_in(key, axis), (), 0, length) for axis, length in enumerate(array.shape)]
    main_axis = array.shape.index(max(array.shape))
    next_to = index_at[:main_axis] + [(index_at[main_axis] + 1) % array.shape[main_axis]] + index_at[main_axis + 1:]
    return array.at[tuple(index_at)].set(least).at[tuple(next_to)].set(largest)


def level_of(own_key, extent, cuts, least, top_value):
    def one(dim, parts):
        heights = jax.random.uniform(jax.random.fold_in(jax.random.fold_in(own_key, 6), dim), (parts,), jnp.float32, least / len(cuts), top_value / len(cuts))
        return jnp.repeat(jnp.exp(heights), extent[dim] // parts).reshape((-1,) + (1,) * (len(extent) - dim - 1))

    level = one(*cuts[0])
    for cut in cuts[1:]:
        level = level * one(*cut)
    return level


def normal_values(rng, extent, spread, reach, split=(), kind=jnp.bfloat16):
    drawn = jax.random.normal(rng, extent, jnp.float32) * spread
    if len(split) > 0:
        drawn = level_of(rng, extent, split, -0.22, 0.18) * drawn
    return jnp.clip(drawn, min=-reach, max=reach).astype(kind)


def setup_inputs(seed: int = 0) -> dict:
    key_list = jax.random.split(jax.random.key(seed), 9)
    return {
        "states": normal_values(key_list[0], (N_LEAD, MB, C, NY, NX), 1.0, 6.0, ((0, 2), (3, 16)), jnp.float32),
        "cotangents": normal_values(key_list[1], (N_LEAD, MB, C, NY, NX), 1.0, 6.0, ((0, 2), (3, 16)), jnp.float32),
        "w_conv": normal_values(key_list[2], (9 * C, H), (9 * C) ** -0.5, 0.1875),
        "b_conv": normal_values(key_list[3], (H,), 0.5, 3.0, (), jnp.float32),
        "w_out": normal_values(key_list[4], (H, C), H ** -0.5, 0.25),
        "forcing": normal_values(key_list[5], (DAYS, C), 0.5, 3.0, (), jnp.float32),
        "land": place_ends((jax.random.randint(key_list[6], (NY, NX), 0, 10) < 7).astype(jnp.int32), jax.random.fold_in(key_list[6], 1), 0, 1),
        "dates": jax.random.randint(key_list[7], (MB,), 0, DAYS).astype(jnp.int32),
    }


TANH_SCALE = 0.7978845608028654
CUBIC_TERM = 0.044715
OFFSETS = [(-1, -1), (-1, 0), (-1, 1), (0, -1), (0, 0), (0, 1), (1, -1), (1, 0), (1, 1)]

def gelu_pair(values):
    tanh_value = jnp.tanh(TANH_SCALE * (values + CUBIC_TERM * values * values * values))
    output = 0.5 * values * (1.0 + tanh_value)
    gelu_slope = 0.5 * (1.0 + tanh_value) + 0.5 * values * (1.0 - tanh_value * tanh_value) * TANH_SCALE * (1.0 + 3.0 * CUBIC_TERM * values * values)
    return (output, gelu_slope)

def matmul_full(left, right):
    return jnp.dot(left.astype(jnp.float32), right.astype(jnp.float32), precision=lax.Precision.HIGHEST, preferred_element_type=jnp.float32)

def member_grad(state_field, total_grad, shift_row, w_conv, b_conv, w_out, land_cols):
    channels, lat_rows, lon_cols = state_field.shape
    hidden_width = w_conv.shape[1]
    columns = lat_rows * lon_cols
    rounded = (state_field + shift_row[:, None, None]).astype(jnp.bfloat16)
    padded = jnp.pad(rounded, ((0, 0), (1, 1), (0, 0)))
    preact = jnp.zeros((hidden_width, columns), jnp.float32) + b_conv[:, None]
    tap_views = []
    for offset, (row_step, col_step) in enumerate(OFFSETS):
        tap_view = jnp.roll(padded[:, 1 + row_step:1 + row_step + lat_rows, :], -col_step, axis=2).reshape(channels, columns)
        tap_views.append(tap_view)
        tap_block = w_conv[offset * channels:(offset + 1) * channels]
        preact = preact + matmul_full(tap_block.T, tap_view)
    output, gelu_slope = gelu_pair(preact)
    hidden = output.astype(jnp.bfloat16)
    masked = (land_cols[None] * total_grad).astype(jnp.bfloat16).reshape(channels, columns)
    hidden_grad = matmul_full(w_out, masked)
    pre_grad = hidden_grad * gelu_slope
    pre_round = pre_grad.astype(jnp.bfloat16)
    w2_part = matmul_full(hidden, masked.T)
    bias_part = lax.optimization_barrier(jnp.sum(pre_grad, axis=1))
    w1_part = jnp.concatenate([matmul_full(tap_view, pre_round.T) for tap_view in tap_views], axis=0)
    input_grad = jnp.zeros((channels, lat_rows, lon_cols), jnp.float32)
    for offset, (row_step, col_step) in enumerate(OFFSETS):
        tap_block = w_conv[offset * channels:(offset + 1) * channels]
        tap_term = matmul_full(tap_block, pre_round).reshape(channels, lat_rows, lon_cols)
        tap_term = jnp.pad(tap_term, ((0, 0), (1, 1), (0, 0)))
        input_grad = input_grad + jnp.roll(tap_term[:, 1 - row_step:1 - row_step + lat_rows, :], col_step, axis=2)
    return (total_grad + input_grad, w1_part, w2_part, bias_part)

def reference(states, cotangents, w_conv, b_conv, w_out, forcing, land, dates):
    section_count = states.shape[0]
    member_count = states.shape[1]
    day_count = forcing.shape[0]
    land_cols = land.astype(jnp.float32)
    w1_total = jnp.zeros(w_conv.shape, jnp.float32)
    w2_total = jnp.zeros(w_out.shape, jnp.float32)
    bias_total = jnp.zeros(b_conv.shape, jnp.float32)
    incoming = jnp.zeros(states.shape[1:], jnp.float32)
    results = [None] * section_count
    for section_index in reversed(range(section_count)):
        day_index = ((dates + section_index) % day_count).astype(jnp.int32)
        picked = (jnp.arange(day_count, dtype=jnp.int32)[None, :] == day_index[:, None]).astype(jnp.float32)
        shifts = jnp.dot(picked, forcing, precision=lax.Precision.HIGHEST, preferred_element_type=jnp.float32)
        totals = cotangents[section_index] + incoming
        member_list = []
        for member in range(member_count):
            member_grads, w1_part, w2_part, bias_part = member_grad(states[section_index, member], totals[member], shifts[member], w_conv, b_conv, w_out, land_cols)
            member_list.append(member_grads)
            w1_total = w1_total + w1_part
            w2_total = w2_total + w2_part
            bias_total = bias_total + bias_part
        results[section_index] = jnp.stack(member_list)
        incoming = results[section_index]
    grad_scale = 1.0 / math.sqrt(section_count * member_count * land.shape[0] * land.shape[1])
    return (jnp.stack(results), w1_total * grad_scale, w2_total * grad_scale, bias_total * grad_scale)
```

```python
import functools
import math

import jax
import jax.numpy as jnp
from jax import lax
from jax.experimental import pallas as pl
from jax.experimental.pallas import tpu as pltpu
from jax.sharding import PartitionSpec as P

TANH_SCALE = 0.7978845608028654
CUBIC_TERM = 0.044715
BF16 = jnp.bfloat16
F32 = jnp.float32
WHOLE = pl.BlockSpec(memory_space=pltpu.VMEM)


def dot(left, right):
    return jnp.dot(left, right, preferred_element_type=F32)


def dot_t(left, right):
    return lax.dot_general(left, right, (((1,), (1,)), ((), ())), preferred_element_type=F32)


def gelu_pair(v):
    square = v * v
    t = jnp.tanh(TANH_SCALE * (v + CUBIC_TERM * (square * v)))
    half = 0.5 * (1.0 + t)
    slope = half + (0.5 * v) * (1.0 - t * t) * (TANH_SCALE * (1.0 + 3.0 * CUBIC_TERM * square))
    return v * half, slope


def member_block(shape, member):
    rest = len(shape) - 1
    return pl.BlockSpec((1,) + tuple(shape[1:]), lambda i: (member,) + (0,) * rest)


def full_block(shape):
    return pl.BlockSpec(tuple(shape), lambda i: (0,) * len(shape))


def prep_body(rows, dates, section, forcing, states, rounded, top, bottom):
    m = pl.program_id(0)
    days, channels = forcing.shape
    lon = states.shape[2]
    day = (dates[m] + section[0]) % days
    line = forcing[pl.ds(day, 1), :]
    shift = jnp.broadcast_to(line, (lon, channels)).T
    for r in range(rows):
        value = (states[0, pl.ds(r, channels, stride=rows), :] + shift).astype(BF16)
        rounded[0, r] = value
        if r == 0:
            top[0] = value
        if r == rows - 1:
            bottom[0] = value


def prep(dates, section, forcing, states, rows):
    members, flat, lon = states.shape
    channels = flat // rows
    smem = pl.BlockSpec(memory_space=pltpu.SMEM)
    return pl.pallas_call(
        functools.partial(prep_body, rows),
        grid=(members,),
        in_specs=[
            smem,
            smem,
            full_block(forcing.shape),
            pl.BlockSpec((1, flat, lon), lambda m: (m, 0, 0)),
        ],
        out_specs=[
            pl.BlockSpec((1, rows, channels, lon), lambda m: (m, 0, 0, 0)),
            pl.BlockSpec((1, channels, lon), lambda m: (m, 0, 0)),
            pl.BlockSpec((1, channels, lon), lambda m: (m, 0, 0)),
        ],
        out_shape=[
            jax.ShapeDtypeStruct((members, rows, channels, lon), BF16),
            jax.ShapeDtypeStruct((members, channels, lon), BF16),
            jax.ShapeDtypeStruct((members, channels, lon), BF16),
        ],
        name="prep",
    )(dates, section, forcing, states)


def turn_body(w_conv, b_conv, turned, column):
    turned[...] = w_conv[...].T
    column[...] = jnp.broadcast_to(b_conv[...], (column.shape[1], column.shape[0])).T


def turn(w_conv, b_conv, lanes):
    taps, hidden = w_conv.shape
    return pl.pallas_call(
        turn_body,
        out_shape=[
            jax.ShapeDtypeStruct((hidden, taps), BF16),
            jax.ShapeDtypeStruct((hidden, lanes), F32),
        ],
        name="turn",
    )(w_conv, b_conv)


def spread_grad(w_conv, pre, z, channels, rows, lon):
    for k in range(0, rows, 2):
        cols = slice(k * lon, (k + 2) * lon)
        z[:, cols] = dot(w_conv[...], pre[:, cols])
    out = []
    for i in range(-1, rows + 1):
        per_step = []
        for cs in range(3):
            total = None
            for rs in range(3):
                source = i - (rs - 1)
                if 0 <= source < rows:
                    tap = 3 * rs + cs
                    term = z[tap * channels : (tap + 1) * channels, source * lon : (source + 1) * lon]
                    total = term if total is None else total + term
            per_step.append(total)
        out.append(
            per_step[1] + pltpu.roll(per_step[0], lon - 1, 1) + pltpu.roll(per_step[2], 1, 1)
        )
    return out


def total_row(r, rows, channels, cot, coming):
    total = cot[0, pl.ds(r, channels, stride=rows), :]
    if coming is not None:
        main, low, high = coming
        total = total + main[r].astype(F32)
        if r == 0:
            total = total + low[...].astype(F32)
        if r == rows - 1:
            total = total + high[...].astype(F32)
    return total


def forward_body(
    rounded, low, high, turned, column, w_conv, w_out, cot, land,
    stack, hidden, slope, main, up, down, masked, pre, z,
):
    _, rows, channels, lon = rounded.shape
    for q in range(rows + 2):
        if q == 0:
            x = low[0]
        elif q == rows + 1:
            x = high[0]
        else:
            x = rounded[0, q - 1]
        wide = x.astype(F32)
        at = slice(q * lon, (q + 1) * lon)
        stack[0:channels, at] = pltpu.roll(wide, 1, 1).astype(BF16)
        stack[channels : 2 * channels, at] = x
        stack[2 * channels : 3 * channels, at] = pltpu.roll(wide, lon - 1, 1).astype(BF16)
    for r in range(rows):
        total = total_row(r, rows, channels, cot, None)
        masked[:, r * lon : (r + 1) * lon] = (land[r : r + 1, :].astype(F32) * total).astype(BF16)
    bias = jnp.concatenate([column[...], column[...]], axis=1)
    for k in range(0, rows, 2):
        preact = bias
        for rs in range(3):
            preact = preact + dot(
                turned[:, rs * 3 * channels : (rs + 1) * 3 * channels],
                stack[:, (k + rs) * lon : (k + rs + 2) * lon],
            )
        value, steep = gelu_pair(preact)
        cols = slice(k * lon, (k + 2) * lon)
        hidden[:, cols] = value.astype(BF16)
        slope[:, cols] = steep.astype(BF16)
        pre[:, cols] = (dot(w_out[...], masked[:, cols]) * steep).astype(BF16)
    grads = spread_grad(w_conv, pre, z, channels, rows, lon)
    up[...] = grads[0].astype(BF16)
    down[...] = grads[rows + 1].astype(BF16)
    for r in range(rows):
        main[r] = (grads[r + 1] + total_row(r, rows, channels, cot, None)).astype(BF16)


def forward(member, rounded, low, high, turned, column, w_conv, w_out, cot, land):
    _, rows, channels, lon = rounded.shape
    taps, width = w_conv.shape
    cols = rows * lon
    operands = (rounded, low, high, turned, column, w_conv, w_out, cot, land)
    specs = [member_block(rounded.shape, member), member_block(low.shape, member), member_block(high.shape, member)]
    specs += [full_block(x.shape) for x in (turned, column, w_conv, w_out)]
    specs += [member_block(cot.shape, member), full_block(land.shape)]
    shapes = [
        ((3 * channels, (rows + 2) * lon), BF16),
        ((width, cols), BF16),
        ((width, cols), BF16),
        ((rows, channels, lon), BF16),
        ((channels, lon), BF16),
        ((channels, lon), BF16),
    ]
    return pl.pallas_call(
        forward_body,
        grid=(1,),
        in_specs=specs,
        out_specs=[full_block(s) for s, _ in shapes],
        out_shape=[jax.ShapeDtypeStruct(s, d) for s, d in shapes],
        scratch_shapes=[
            pltpu.VMEM((channels, cols), BF16),
            pltpu.VMEM((width, cols), BF16),
            pltpu.VMEM((taps, cols), F32),
        ],
        name=f"forward_{member}",
    )(*operands)


def weight_body(first, last, parts, *refs):
    cot, land, w_out, hidden, slope, stack, main, low, high = refs[:9]
    refs = refs[9:]
    if not first:
        w1_in, w2_in, b_in = refs[:3]
        refs = refs[3:]
    if last:
        packed, pre, masked, w1, w2, sums = refs
    else:
        w1, w2, sums, pre, masked = refs
    rows, channels, lon = main.shape
    width = w_out.shape[0]
    for r in range(rows):
        total = total_row(r, rows, channels, cot, (main, low, high))
        masked[:, r * lon : (r + 1) * lon] = (land[r : r + 1, :].astype(F32) * total).astype(BF16)
    acc = jnp.zeros((width, lon), F32) if first else b_in[...]
    for k in range(0, rows, 2):
        cols = slice(k * lon, (k + 2) * lon)
        grad = dot(w_out[...], masked[:, cols]) * slope[:, cols].astype(F32)
        pre[:, cols] = grad.astype(BF16)
        acc = acc + (grad[:, :lon] + grad[:, lon:])
    for rs in range(3):
        at = slice(rs * 3 * channels, (rs + 1) * 3 * channels)
        part = dot_t(stack[:, rs * lon : (rs + rows) * lon], pre[...])
        w1[at, :] = part if first else part + w1_in[at, :]
    part = dot_t(hidden[...], masked[...])
    w2[...] = part if first else part + w2_in[...]
    if not last:
        sums[...] = acc
        return
    line = jnp.sum(acc.T, axis=0, keepdims=True)
    deep, wide = w1.shape[0] // parts, width // parts
    folds = width // channels
    thin = wide // folds
    for t in range(parts):
        packed[t, 0:deep, :] = w1[t * deep : (t + 1) * deep, :]
        for f in range(folds):
            packed[t, deep : deep + thin, f * channels : (f + 1) * channels] = w2[
                t * wide + f * thin : t * wide + (f + 1) * thin, :
            ]
        packed[t, deep + thin : deep + thin + 1, :] = pltpu.roll(line, (width - t * wide) % width, 1)


def packed_rows(taps, width, channels, parts):
    used = taps // parts + width // parts // (width // channels) + 1
    return -(-used // 8) * 8


def weight(member, last, parts, cot, land, w_out, hidden, slope, stack, coming, before):
    rows, channels, lon = coming[0].shape
    width = w_out.shape[0]
    cols = rows * lon
    taps = 3 * stack.shape[0]
    first = before is None
    operands = [cot, land, w_out, hidden, slope, stack, *coming]
    specs = [member_block(cot.shape, member)] + [full_block(x.shape) for x in operands[1:]]
    if not first:
        operands += list(before)
        specs += [full_block(x.shape) for x in before]
    sums = [((taps, width), F32), ((width, channels), F32), ((width, lon), F32)]
    if last:
        shapes = [((parts, packed_rows(taps, width, channels, parts), width), F32), ((width, cols), BF16)]
        scratch = [pltpu.VMEM((channels, cols), BF16)] + [pltpu.VMEM(s, d) for s, d in sums]
    else:
        shapes = sums + [((width, cols), BF16)]
        scratch = [pltpu.VMEM((channels, cols), BF16)]
    return pl.pallas_call(
        functools.partial(weight_body, first, last, parts),
        grid=(1,),
        in_specs=specs,
        out_specs=[full_block(s) for s, _ in shapes],
        out_shape=[jax.ShapeDtypeStruct(s, d) for s, d in shapes],
        scratch_shapes=scratch,
        name=f"weight_{member}",
    )(*operands)


def state_body(pre, w_conv, cot, main, low, high, out, up, down, z):
    rows, channels, lon = main.shape
    grads = spread_grad(w_conv, pre, z, channels, rows, lon)
    up[...] = grads[0].astype(BF16)
    down[...] = grads[rows + 1].astype(BF16)
    for r in range(rows):
        out[pl.ds(r, channels, stride=rows), :] = grads[r + 1] + total_row(
            r, rows, channels, cot, (main, low, high)
        )


def state_grad(member, pre, w_conv, cot, coming):
    rows, channels, lon = coming[0].shape
    operands = [pre, w_conv, cot, *coming]
    specs = [full_block(x.shape) for x in operands]
    specs[2] = member_block(cot.shape, member)
    shapes = [((rows * channels, lon), F32), ((channels, lon), BF16), ((channels, lon), BF16)]
    return pl.pallas_call(
        state_body,
        grid=(1,),
        in_specs=specs,
        out_specs=[full_block(s) for s, _ in shapes],
        out_shape=[jax.ShapeDtypeStruct(s, d) for s, d in shapes],
        scratch_shapes=[pltpu.VMEM((w_conv.shape[0], rows * lon), F32)],
        name=f"state_{member}",
    )(*operands)


def join_body(rows, *refs):
    members = (len(refs) - 1) // 3
    out = refs[-1]
    channels = refs[1].shape[0]
    for m in range(members):
        body, low, high = refs[3 * m : 3 * m + 3]
        for r in range(rows):
            at = pl.ds(r, channels, stride=rows)
            value = body[at, :]
            if r == 0:
                value = value + low[...].astype(F32)
            if r == rows - 1:
                value = value + high[...].astype(F32)
            out[m, at, :] = value


def join(rows, pieces):
    flat, lon = pieces[0][0].shape
    return pl.pallas_call(
        functools.partial(join_body, rows),
        out_shape=jax.ShapeDtypeStruct((len(pieces), flat, lon), F32),
        name="join",
    )(*[x for piece in pieces for x in piece])


def summed(packed):
    parts = lax.axis_size("tile")
    leads = lax.axis_size("lead")
    here = lax.axis_index("tile")
    depth = parts.bit_length() - 1
    value = packed.reshape((2,) * depth + packed.shape[1:])
    for k in range(depth):
        dim = depth - 1 - k
        bit = (here >> k) & 1
        keep = lax.dynamic_index_in_dim(value, bit, dim, keepdims=True)
        give = lax.dynamic_index_in_dim(value, 1 - bit, dim, keepdims=True).astype(BF16)
        taken = lax.ppermute(give, "tile", [(t, t ^ (1 << k)) for t in range(parts)])
        value = keep + taken.astype(F32)
    value = value.reshape(packed.shape[1:])
    for k in range(leads.bit_length() - 1):
        taken = lax.ppermute(value.astype(BF16), "lead", [(s, s ^ (1 << k)) for s in range(leads)])
        value = value + taken.astype(F32)
    return value


def shards(states, cotangents, w_conv, b_conv, w_out, forcing, land, dates):
    section = lax.axis_index("lead").astype(jnp.int32)
    leads = lax.axis_size("lead")
    tiles = lax.axis_size("tile")
    _, members, channels, rows, lon = states.shape
    taps, width = w_conv.shape
    own = states.reshape(members, channels * rows, lon)
    cot = cotangents.reshape(members, channels * rows, lon)
    rounded, top, bottom = prep(dates, section[None], forcing, own, rows)
    ahead = [(t, t + 1) for t in range(tiles - 1)]
    behind = [(t + 1, t) for t in range(tiles - 1)]
    low = lax.ppermute(bottom, "tile", ahead)
    high = lax.ppermute(top, "tile", behind)
    turned, column = turn(w_conv, b_conv[None, :], lon)

    def to_previous(main, up, down):
        pair = ("lead", "tile")
        steps = [(s, s - 1) for s in range(1, leads)]
        return (
            lax.ppermute(main, "lead", steps),
            lax.ppermute(down, pair, [(s * tiles + a, d * tiles + b) for s, d in steps for a, b in ahead]),
            lax.ppermute(up, pair, [(s * tiles + a, d * tiles + b) for s, d in steps for a, b in behind]),
        )

    kept = []
    for m in range(members):
        stack, hidden, slope, *grads = forward(
            m, rounded, low, high, turned, column, w_conv, w_out, cot, land
        )
        kept.append((stack, hidden, slope, to_previous(*grads)))
    before = None
    pieces = []
    for m in range(members):
        stack, hidden, slope, coming = kept[m]
        last = m + 1 == members
        *sums, pre = weight(m, last, tiles, cot, land, w_out, hidden, slope, stack, coming, before)
        before = sums
        body, up, down = state_grad(m, pre, w_conv, cot, coming)
        pieces.append((body, lax.ppermute(down, "tile", ahead), lax.ppermute(up, "tile", behind)))
    scale = 1.0 / math.sqrt(leads * members * rows * tiles * lon)
    total = summed(before[0]) * scale
    grads = join(rows, pieces).reshape(states.shape)
    deep, wide = taps // tiles, width // tiles
    folds = width // channels
    thin = wide // folds
    w1 = total[:deep]
    w2 = total[deep : deep + thin].reshape(thin, folds, channels).transpose(1, 0, 2).reshape(wide, channels)
    b1 = total[deep + thin, :wide]
    return grads, w1, w2, b1


def solution(mesh):
    assert mesh.shape["lead"] == 2
    placed = (
        P("lead", None, None, "tile", None),
        P("lead", None, None, "tile", None),
        P(),
        P(),
        P(),
        P(),
        P("tile", None),
        P(),
    )
    return jax.shard_map(
        shards,
        mesh=mesh,
        in_specs=placed,
        out_specs=(
            P("lead", None, None, "tile", None),
            P("tile", None),
            P("tile", None),
            P("tile"),
        ),
        check_vma=False,
    )
```

```python
import functools
import math

import jax
import jax.numpy as jnp
from jax import lax
from jax.experimental import pallas as pl
from jax.experimental.pallas import tpu as pltpu
from jax.sharding import PartitionSpec as P

TANH_SCALE = 0.7978845608028654
CUBIC_TERM = 0.044715
BF16 = jnp.bfloat16
F32 = jnp.float32
PARAMS = pltpu.CompilerParams(vmem_limit_bytes=32 * 1024 * 1024)


def dot(left, right):
    return jnp.dot(left, right, preferred_element_type=F32)


def dot_t(left, right):
    return lax.dot_general(left, right, (((1,), (1,)), ((), ())), preferred_element_type=F32)


def gelu_pair(v):
    square = v * v
    t = jnp.tanh(TANH_SCALE * (v + CUBIC_TERM * (square * v)))
    half = 0.5 * (1.0 + t)
    slope = half + (0.5 * v) * (1.0 - t * t) * (TANH_SCALE * (1.0 + 3.0 * CUBIC_TERM * square))
    return v * half, slope


def member_block(shape, member):
    rest = len(shape) - 1
    return pl.BlockSpec((1,) + tuple(shape[1:]), lambda i: (member,) + (0,) * rest)


def full_block(shape):
    return pl.BlockSpec(tuple(shape), lambda i: (0,) * len(shape))


def prep_body(rows, dates, section, forcing, states, cot, land, rounded, top, bottom):
    m = pl.program_id(0)
    days, channels = forcing.shape
    lon = states.shape[2]
    day = (dates[m] + section[0]) % days
    line = forcing[pl.ds(day, 1), :]
    shift = jnp.broadcast_to(line, (lon, channels)).T
    for r in range(rows):
        value = (states[0, pl.ds(r, channels, stride=rows), :] + shift).astype(BF16)
        rounded[0, r] = value
        if r < 2:
            top[0, r] = value
        if r >= rows - 2:
            bottom[0, r - (rows - 2)] = value
    top[0, 2] = masked_row(0, channels, cot, land, total_row(0, rows, channels, cot, 0))
    bottom[0, 2] = masked_row(rows - 1, channels, cot, land, total_row(rows - 1, rows, channels, cot, 0))


def prep(dates, section, forcing, states, cot, land):
    members, flat, lon = states.shape
    rows = land.shape[0]
    channels = flat // rows
    smem = pl.BlockSpec(memory_space=pltpu.SMEM)
    own = pl.BlockSpec((1, flat, lon), lambda m: (m, 0, 0))
    halo = pl.BlockSpec((1, 3, channels, lon), lambda m: (m, 0, 0, 0))
    return pl.pallas_call(
        functools.partial(prep_body, rows),
        grid=(members,),
        in_specs=[smem, smem, full_block(forcing.shape), own, own, full_block(land.shape)],
        out_specs=[pl.BlockSpec((1, rows, channels, lon), lambda m: (m, 0, 0, 0)), halo, halo],
        out_shape=[
            jax.ShapeDtypeStruct((members, rows, channels, lon), BF16),
            jax.ShapeDtypeStruct((members, 3, channels, lon), BF16),
            jax.ShapeDtypeStruct((members, 3, channels, lon), BF16),
        ],
        name="prep",
    )(dates, section, forcing, states, cot, land)


def turn_body(w_conv, b_conv, turned, column):
    turned[...] = w_conv[...].T
    column[...] = jnp.broadcast_to(b_conv[...], (column.shape[1], column.shape[0])).T


def turn(w_conv, b_conv, lanes):
    taps, hidden = w_conv.shape
    return pl.pallas_call(
        turn_body,
        out_shape=[
            jax.ShapeDtypeStruct((hidden, taps), BF16),
            jax.ShapeDtypeStruct((hidden, lanes), F32),
        ],
        compiler_params=PARAMS,
        name="turn",
    )(w_conv, b_conv)


def edge_grads(w_conv, pre, channels, rows, lon):
    out = []
    for rs, source in ((0, 0), (2, rows - 1)):
        block = w_conv[rs * 3 * channels : (rs + 1) * 3 * channels, :]
        part = dot(block, pre[:, source * lon : (source + 1) * lon])
        out.append(
            part[channels : 2 * channels]
            + pltpu.roll(part[:channels], lon - 1, 1)
            + pltpu.roll(part[2 * channels :], 1, 1)
        )
    return out


def own_grads(w_conv, pre, z, channels, rows, lon, halo):
    taps = 9 * channels
    for k in range(0, rows, 2):
        cols = slice((k + halo) * lon, (k + halo + 2) * lon)
        z[0:taps, cols] = dot(w_conv[...], pre[:, cols])
    for source, rs in ((-1, 2), (rows, 0)) if halo else ():
        cols = slice((source + 1) * lon, (source + 2) * lon)
        block = slice(rs * 3 * channels, (rs + 1) * 3 * channels)
        z[block, cols] = dot(w_conv[block, :], pre[:, cols])
    for i in range(rows):
        per_step = []
        for cs in range(3):
            total = None
            for rs in range(3):
                source = i - (rs - 1)
                if -halo <= source < rows + halo:
                    tap = 3 * rs + cs
                    at = (source + halo) * lon
                    term = z[tap * channels : (tap + 1) * channels, at : at + lon]
                    total = term if total is None else total + term
            per_step.append(total)
        yield per_step[1] + pltpu.roll(per_step[0], lon - 1, 1) + pltpu.roll(per_step[2], 1, 1)


def total_row(r, rows, channels, cot, member, main=None):
    total = cot[member, pl.ds(r, channels, stride=rows), :]
    return total if main is None else total + main[r].astype(F32)


def masked_row(r, channels, cot, land, total):
    return (land[r : r + 1, :].astype(F32) * total).astype(BF16)


def build_stack(rounded, low, high, stack, member, halo):
    _, rows, channels, lon = rounded.shape
    for q in range(-halo, rows + halo):
        if q < 0:
            x = low[member, 2 + q]
        elif q >= rows:
            x = high[member, q - rows]
        else:
            x = rounded[member, q]
        wide = x.astype(F32)
        at = slice((q + halo) * lon, (q + halo + 1) * lon)
        stack[0:channels, at] = pltpu.roll(wide, 1, 1).astype(BF16)
        stack[channels : 2 * channels, at] = x
        stack[2 * channels : 3 * channels, at] = pltpu.roll(wide, lon - 1, 1).astype(BF16)


def forward_body(
    rounded, low, high, turned, column, w_conv, w_out, cot, land,
    main, hidden_out, slope_out, stack, hidden, slope, masked, pre, z, sems,
):
    _, rows, channels, lon = rounded.shape
    build_stack(rounded, low, high, stack, 0, 2)
    masked[:, 0:lon] = low[0, 2]
    for r in range(rows):
        masked[:, (r + 1) * lon : (r + 2) * lon] = masked_row(
            r, channels, cot, land, total_row(r, rows, channels, cot, 0)
        )
    masked[:, (rows + 1) * lon :] = high[0, 2]
    bias = jnp.concatenate([column[...], column[...]], axis=1)
    for k in range(0, rows + 2, 2):
        preact = bias
        for rs in range(3):
            preact = preact + dot(
                turned[:, rs * 3 * channels : (rs + 1) * 3 * channels],
                stack[:, (k + rs) * lon : (k + rs + 2) * lon],
            )
        value, steep = gelu_pair(preact)
        cols = slice(k * lon, (k + 2) * lon)
        hidden[:, cols] = value.astype(BF16)
        slope[:, cols] = steep
        pre[:, cols] = (dot(w_out[...], masked[:, cols]) * steep).astype(BF16)
    inner = slice(lon, (rows + 1) * lon)
    copies = [
        pltpu.make_async_copy(hidden.at[:, inner], hidden_out, sems.at[0]),
        pltpu.make_async_copy(slope.at[:, inner], slope_out, sems.at[1]),
    ]
    for copy in copies:
        copy.start()
    for r, grad in enumerate(own_grads(w_conv, pre, z, channels, rows, lon, 1)):
        main[r] = (grad + total_row(r, rows, channels, cot, 0)).astype(BF16)
    for copy in copies:
        copy.wait()


def forward(member, rounded, low, high, turned, column, w_conv, w_out, cot, land):
    _, rows, channels, lon = rounded.shape
    taps, width = w_conv.shape
    cols, more = rows * lon, (rows + 2) * lon
    operands = [rounded, low, high, turned, column, w_conv, w_out, cot, land]
    specs = [member_block(x.shape, member) for x in (rounded, low, high)]
    specs += [full_block(x.shape) for x in (turned, column, w_conv, w_out)]
    specs += [member_block(cot.shape, member), full_block(land.shape)]
    main = (rows, channels, lon)
    hbm = pl.BlockSpec(memory_space=pltpu.HBM)
    return pl.pallas_call(
        forward_body,
        grid=(1,),
        in_specs=specs,
        out_specs=[full_block(main), hbm, hbm],
        out_shape=[jax.ShapeDtypeStruct(main, BF16), pltpu.HBM((width, cols), BF16), pltpu.HBM((width, cols), F32)],
        scratch_shapes=[
            pltpu.VMEM((3 * channels, (rows + 4) * lon), BF16),
            pltpu.VMEM((width, more), BF16),
            pltpu.VMEM((width, more), F32),
            pltpu.VMEM((channels, more), BF16),
            pltpu.VMEM((width, more), BF16),
            pltpu.VMEM((taps, more), F32),
            pltpu.SemaphoreType.DMA((2,)),
        ],
        compiler_params=PARAMS,
        name=f"forward_{member}",
    )(*operands)


def phase_bits(parts, core):
    bits = list(range(parts.bit_length() - 1))
    if len(bits) > 2 and core == 1:
        bits[1], bits[2] = bits[2], bits[1]
    return bits


def place_of(relative, core, parts):
    even, odd = phase_bits(parts, 0), phase_bits(parts, 1)
    depth = len(even)
    place = 0
    for i in range(1, depth):
        bit = (relative >> even[i]) & 1
        if even[i] != odd[i]:
            bit = jnp.where(core == 0, bit, (relative >> odd[i]) & 1)
        place = place + (bit << (depth - 1 - i))
    return place


def weight_body(members, parts, here_ref, rounded, low, high, cot, land, w_out, w_conv, *refs):
    mains, held = refs[:members], refs[members : 3 * members]
    give, keep, up, down = refs[3 * members : 3 * members + 4]
    pres = refs[3 * members + 4 : 4 * members + 4]
    refs = refs[4 * members + 4 :]
    local = refs[: 2 * members]
    stack, masked, w1, w2, sems = refs[2 * members :]
    _, rows, channels, lon = rounded.shape
    width = w_out.shape[0]
    cols = rows * lon
    copies = [pltpu.make_async_copy(a, b, sems.at[i]) for i, (a, b) in enumerate(zip(held, local))]
    for copy in copies:
        copy.start()
    acc = None
    for m in range(members):
        hidden, slope = local[2 * m : 2 * m + 2]
        build_stack(rounded, low, high, stack.at[m], m, 1)
        for r in range(rows):
            masked[m, :, r * lon : (r + 1) * lon] = masked_row(
                r, channels, cot, land, total_row(r, rows, channels, cot, m, mains[m])
            )
        copies[2 * m].wait()
        part = dot_t(hidden[...], masked[m])
        w2[...] = part if m == 0 else part + w2[...]
        copies[2 * m + 1].wait()
        for k in range(0, rows, 2):
            at = slice(k * lon, (k + 2) * lon)
            grad = dot(w_out[...], masked[m, :, at]) * slope[:, at]
            pres[m][:, at] = grad.astype(BF16)
            both = grad[:, :lon] + grad[:, lon:]
            acc = both if acc is None else acc + both
        above, below = edge_grads(w_conv, pres[m], channels, rows, lon)
        up[m] = above.astype(BF16)
        down[m] = below.astype(BF16)
        for rs in range(3):
            at = slice(rs * 3 * channels, (rs + 1) * 3 * channels)
            part = dot_t(stack[m, :, rs * lon : rs * lon + cols], pres[m][...])
            w1[at, :] = part if m == 0 else part + w1[at, :]

    here = here_ref[0]
    core = here & 1
    line = jnp.sum(acc.T, axis=0, keepdims=True)
    deep, wide = w1.shape[0] // parts, width // parts
    folds = width // channels
    thin = wide // folds

    def fill(target, place, t):
        kind = target.dtype
        target[place, 0:deep, :] = w1[t * deep : (t + 1) * deep, :].astype(kind)
        for f in range(folds):
            target[place, deep : deep + thin, f * channels : (f + 1) * channels] = w2[
                t * wide + f * thin : t * wide + (f + 1) * thin, :
            ].astype(kind)
        shifted = line if t == 0 else pltpu.roll(line, width - t * wide, 1)
        target[place, deep + thin : deep + thin + 1, :] = shifted.astype(kind)

    for t in range(parts):
        relative = here ^ t

        @pl.when((relative & 1) == 0)
        def _():
            fill(keep, place_of(relative, core, parts), t)

        @pl.when((relative & 1) == 1)
        def _():
            fill(give, place_of(relative, 1 - core, parts), t)


def packed_rows(taps, width, channels, parts):
    used = taps // parts + width // parts // (width // channels) + 1
    return -(-used // 8) * 8


def weight(here, parts, rounded, low, high, cot, land, w_out, w_conv, mains, kept):
    members, rows, channels, lon = rounded.shape
    taps, width = w_conv.shape
    cols = rows * lon

    def full(shape):
        return pl.BlockSpec(tuple(shape), lambda i, _: (0,) * len(shape))

    operands = [rounded, low, high, cot, land, w_out, w_conv, *mains]
    specs = [full(x.shape) for x in operands]
    held = [x for row in kept for x in row]
    operands += [pltpu.with_memory_space_constraint(x, pltpu.HBM) for x in held]
    specs += [pl.BlockSpec(memory_space=pltpu.HBM) for _ in held]
    chunk = (parts // 2, packed_rows(taps, width, channels, parts), width)
    edge = (members, channels, lon)
    shapes = [(chunk, BF16), (chunk, F32), (edge, BF16), (edge, BF16)] + [((width, cols), BF16)] * members
    return pl.pallas_call(
        functools.partial(weight_body, members, parts),
        grid_spec=pltpu.PrefetchScalarGridSpec(
            num_scalar_prefetch=1,
            grid=(1,),
            in_specs=specs,
            out_specs=[full(s) for s, _ in shapes],
            scratch_shapes=[pltpu.VMEM(x.shape, x.dtype) for x in held]
            + [
                pltpu.VMEM((members, 3 * channels, (rows + 2) * lon), BF16),
                pltpu.VMEM((members, channels, cols), BF16),
                pltpu.VMEM((taps, width), F32),
                pltpu.VMEM((width, channels), F32),
                pltpu.SemaphoreType.DMA((len(held),)),
            ],
        ),
        out_shape=[jax.ShapeDtypeStruct(s, d) for s, d in shapes],
        compiler_params=PARAMS,
        name="weight",
    )(here, *operands)


def state_body(members, w_conv, cot, beside_low, beside_high, *refs):
    pres, mains = refs[:members], refs[members : 2 * members]
    out, z = refs[2 * members :]
    rows, channels, lon = mains[0].shape
    for m in range(members):
        for r, grad in enumerate(own_grads(w_conv, pres[m], z.at[m % 2], channels, rows, lon, 0)):
            total = grad + total_row(r, rows, channels, cot, m, mains[m])
            if r == 0:
                total = total + beside_low[m].astype(F32)
            if r == rows - 1:
                total = total + beside_high[m].astype(F32)
            out[m, pl.ds(r, channels, stride=rows), :] = total


def state_grad(w_conv, cot, beside_low, beside_high, pres, mains):
    taps = w_conv.shape[0]
    operands = [w_conv, cot, beside_low, beside_high, *pres, *mains]
    return pl.pallas_call(
        functools.partial(state_body, len(pres)),
        grid=(1,),
        in_specs=[full_block(x.shape) for x in operands],
        out_specs=full_block(cot.shape),
        out_shape=jax.ShapeDtypeStruct(cot.shape, F32),
        scratch_shapes=[pltpu.VMEM((2, taps, pres[0].shape[1]), F32)],
        compiler_params=PARAMS,
        name="state",
    )(*operands)


def finish_body(scale, own, taken, w1, w2, b1):
    deep = w1.shape[0]
    wide, channels = w2.shape
    folds = own.shape[2] // channels
    thin = wide // folds
    total = (own[0] + taken[0].astype(F32)) * scale
    w1[...] = total[:deep]
    for f in range(folds):
        w2[f * thin : (f + 1) * thin, :] = total[deep : deep + thin, f * channels : (f + 1) * channels]
    b1[...] = total[deep + thin : deep + thin + 1, :wide]


def finish(scale, own, taken, deep, wide, channels):
    return pl.pallas_call(
        functools.partial(finish_body, scale),
        out_shape=[
            jax.ShapeDtypeStruct((deep, own.shape[2]), F32),
            jax.ShapeDtypeStruct((wide, channels), F32),
            jax.ShapeDtypeStruct((1, wide), F32),
        ],
        compiler_params=PARAMS,
        name="finish",
    )(own, taken)


def shards(states, cotangents, w_conv, b_conv, w_out, forcing, land, dates):
    section = lax.axis_index("lead").astype(jnp.int32)
    here = lax.axis_index("tile").astype(jnp.int32)
    leads = lax.axis_size("lead")
    tiles = lax.axis_size("tile")
    _, members, channels, rows, lon = states.shape
    taps, width = w_conv.shape
    own = states.reshape(members, channels * rows, lon)
    cot = cotangents.reshape(members, channels * rows, lon)
    rounded, top, bottom = prep(dates, section[None], forcing, own, cot, land)
    ahead = [(t, t + 1) for t in range(tiles - 1)]
    behind = [(t + 1, t) for t in range(tiles - 1)]
    low = lax.ppermute(bottom, "tile", ahead)
    high = lax.ppermute(top, "tile", behind)
    turned, column = turn(w_conv, b_conv[None, :], lon)

    steps = [(s, s - 1) for s in range(1, leads)]
    kept = []
    mains = []
    for m in range(members):
        main, hidden, slope = forward(m, rounded, low, high, turned, column, w_conv, w_out, cot, land)
        kept.append((hidden, slope))
        mains.append(lax.ppermute(main, "lead", steps))
    give, keep, up, down, *pres = weight(
        here[None], tiles, rounded, low, high, cot, land, w_out, w_conv, mains, kept
    )

    assert tiles >= 8

    def exchanged(value, step):
        bits = (phase_bits(tiles, 0)[step], phase_bits(tiles, 1)[step])
        return lax.ppermute(value, "tile", [(t, t ^ (1 << bits[t & 1])) for t in range(tiles)])

    depth = tiles.bit_length() - 1
    total = keep + exchanged(give, 0).astype(F32)
    for step in range(1, depth):
        half = total.shape[0] // 2
        send = total[half:].astype(BF16)
        if step == 1:
            send, up, down = lax.optimization_barrier((send, up, down))
            beside_low = lax.ppermute(down, "tile", ahead)
            beside_high = lax.ppermute(up, "tile", behind)
        if step == 2:
            send, beside_low, beside_high = lax.optimization_barrier((send, beside_low, beside_high))
            body = state_grad(w_conv, cot, beside_low, beside_high, pres, mains)
        taken = exchanged(send, step)
        if step == 1:
            taken, beside_low, beside_high = lax.optimization_barrier((taken, beside_low, beside_high))
        if step == 2:
            taken, body = lax.optimization_barrier((taken, body))
        total = total[:half] + taken.astype(F32)
    grads = body.reshape(states.shape)
    taken = lax.ppermute(total.astype(BF16), "lead", [(s, leads - 1 - s) for s in range(leads)])
    scale = 1.0 / math.sqrt(leads * members * rows * tiles * lon)
    w1, w2, b1 = finish(scale, total, taken, taps // tiles, width // tiles, channels)
    return grads, w1, w2, b1[0]


def solution(mesh):
    assert mesh.shape["lead"] == 2
    placed = (
        P("lead", None, None, "tile", None),
        P("lead", None, None, "tile", None),
        P(),
        P(),
        P(),
        P(),
        P("tile", None),
        P(),
    )
    return jax.shard_map(
        shards,
        mesh=mesh,
        in_specs=placed,
        out_specs=(
            P("lead", None, None, "tile", None),
            P("tile", None),
            P("tile", None),
            P("tile"),
        ),
        check_vma=False,
    )
```

```python
import functools
import math

import jax
import jax.numpy as jnp
from jax import lax
from jax.experimental import pallas as pl
from jax.experimental.pallas import tpu as pltpu
from jax.sharding import PartitionSpec as P


TANH_SCALE = 0.7978845608028654
CUBIC_TERM = 0.044715
BF16 = jnp.bfloat16
F32 = jnp.float32
STATE_STEP = 3
PARAMS = pltpu.CompilerParams(vmem_limit_bytes=32 * 1024 * 1024)


def dot(left, right):
    return jnp.dot(left, right, preferred_element_type=F32)


def dot_t(left, right):
    return lax.dot_general(left, right, (((1,), (1,)), ((), ())), preferred_element_type=F32)


def gelu_pair(v):
    square = v * v
    half = 0.5 + 0.5 * jnp.tanh(v * (TANH_SCALE + (TANH_SCALE * CUBIC_TERM) * square))
    value = v * half
    slope = half + value * (1.0 - half) * (2.0 * TANH_SCALE + (6.0 * TANH_SCALE * CUBIC_TERM) * square)
    return value, slope


def full_block(shape):
    return pl.BlockSpec(tuple(shape), lambda i: (0,) * len(shape))


def prep_body(rows, dates, section, forcing, states, cot, land, rounded, top, bottom):
    m = pl.program_id(0)
    days, channels = forcing.shape
    lon = states.shape[2]
    day = (dates[m] + section[0]) % days
    line = forcing[pl.ds(day, 1), :]
    shift = jnp.broadcast_to(line, (lon, channels)).T
    for r in range(rows):
        value = (states[0, pl.ds(r, channels, stride=rows), :] + shift).astype(BF16)
        rounded[0, r] = value
        if r < 2:
            top[0, r] = value
        if r >= rows - 2:
            bottom[0, r - (rows - 2)] = value
    top[0, 2] = masked_row(0, land, total_row(0, rows, channels, cot, 0))
    bottom[0, 2] = masked_row(rows - 1, land, total_row(rows - 1, rows, channels, cot, 0))


def prep(dates, section, forcing, states, cot, land):
    members, flat, lon = states.shape
    rows = land.shape[0]
    channels = flat // rows
    smem = pl.BlockSpec(memory_space=pltpu.SMEM)
    own = pl.BlockSpec((1, flat, lon), lambda m: (m, 0, 0))
    halo = pl.BlockSpec((1, 3, channels, lon), lambda m: (m, 0, 0, 0))
    return pl.pallas_call(
        functools.partial(prep_body, rows),
        grid=(members,),
        in_specs=[smem, smem, full_block(forcing.shape), own, own, full_block(land.shape)],
        out_specs=[pl.BlockSpec((1, rows, channels, lon), lambda m: (m, 0, 0, 0)), halo, halo],
        out_shape=[
            jax.ShapeDtypeStruct((members, rows, channels, lon), BF16),
            jax.ShapeDtypeStruct((members, 3, channels, lon), BF16),
            jax.ShapeDtypeStruct((members, 3, channels, lon), BF16),
        ],
        name="prep",
    )(dates, section, forcing, states, cot, land)


def turn_body(w_conv, b_conv, turned, column):
    turned[...] = w_conv[...].T
    column[...] = jnp.broadcast_to(b_conv[...], (column.shape[1], column.shape[0])).T


def turn(w_conv, b_conv, lanes):
    taps, hidden = w_conv.shape
    return pl.pallas_call(
        turn_body,
        out_shape=[
            jax.ShapeDtypeStruct((hidden, taps), BF16),
            jax.ShapeDtypeStruct((hidden, lanes), F32),
        ],
        compiler_params=PARAMS,
        name="turn",
    )(w_conv, b_conv)


def edge_grads(w_conv, pre, channels, rows, lon):
    out = []
    for rs, source in ((0, 0), (2, rows - 1)):
        block = w_conv[rs * 3 * channels : (rs + 1) * 3 * channels, :]
        part = dot(block, pre[:, source * lon : (source + 1) * lon])
        out.append(
            part[channels : 2 * channels]
            + pltpu.roll(part[:channels], lon - 1, 1)
            + pltpu.roll(part[2 * channels :], 1, 1)
        )
    return out


def own_grads(w_conv, pre, z, channels, rows, lon, halo):
    taps = 9 * channels
    for k in range(0, rows, 2):
        cols = slice((k + halo) * lon, (k + halo + 2) * lon)
        z[0:taps, cols] = dot(w_conv[...], pre[:, cols])
    for source, rs in ((-1, 2), (rows, 0)) if halo else ():
        cols = slice((source + 1) * lon, (source + 2) * lon)
        block = slice(rs * 3 * channels, (rs + 1) * 3 * channels)
        z[block, cols] = dot(w_conv[block, :], pre[:, cols])
    for i in range(rows):
        per_step = []
        for cs in range(3):
            total = None
            for rs in range(3):
                source = i - (rs - 1)
                if -halo <= source < rows + halo:
                    tap = 3 * rs + cs
                    at = (source + halo) * lon
                    term = z[tap * channels : (tap + 1) * channels, at : at + lon]
                    total = term if total is None else total + term
            per_step.append(total)
        yield per_step[1] + pltpu.roll(per_step[0], lon - 1, 1) + pltpu.roll(per_step[2], 1, 1)


def total_row(r, rows, channels, cot, member, main=None):
    total = cot[member, pl.ds(r, channels, stride=rows), :]
    return total if main is None else total + main[r].astype(F32)


def masked_row(r, land, total):
    return (land[r : r + 1, :].astype(F32) * total).astype(BF16)


def build_stack(rounded, low, high, stack, member, halo):
    _, rows, channels, lon = rounded.shape
    for q in range(-halo, rows + halo):
        if q < 0:
            x = low[member, 2 + q]
        elif q >= rows:
            x = high[member, q - rows]
        else:
            x = rounded[member, q]
        wide = x.astype(F32)
        at = slice((q + halo) * lon, (q + halo + 1) * lon)
        stack[0:channels, at] = pltpu.roll(wide, 1, 1).astype(BF16)
        stack[channels : 2 * channels, at] = x
        stack[2 * channels : 3 * channels, at] = pltpu.roll(wide, lon - 1, 1).astype(BF16)


def forward_body(
    member, rounded, low, high, turned, column, w_conv, w_out, cot, land,
    main, hidden_out, slope_out, stack, hidden, slope, masked, pre, z, sems,
):
    _, rows, channels, lon = rounded.shape
    build_stack(rounded, low, high, stack, member, 2)
    masked[:, 0:lon] = low[member, 2]
    for r in range(rows):
        masked[:, (r + 1) * lon : (r + 2) * lon] = masked_row(
            r, land, total_row(r, rows, channels, cot, member)
        )
    masked[:, (rows + 1) * lon :] = high[member, 2]
    bias = jnp.concatenate([column[...], column[...]], axis=1)
    for k in range(0, rows + 2, 2):
        preact = bias
        for rs in range(3):
            preact = preact + dot(
                turned[:, rs * 3 * channels : (rs + 1) * 3 * channels],
                stack[:, (k + rs) * lon : (k + rs + 2) * lon],
            )
        value, steep = gelu_pair(preact)
        cols = slice(k * lon, (k + 2) * lon)
        hidden[:, cols] = value.astype(BF16)
        slope[:, cols] = steep
        pre[:, cols] = (dot(w_out[...], masked[:, cols]) * steep).astype(BF16)
    inner = slice(lon, (rows + 1) * lon)
    copies = [
        pltpu.make_async_copy(hidden.at[:, inner], hidden_out, sems.at[0]),
        pltpu.make_async_copy(slope.at[:, inner], slope_out, sems.at[1]),
    ]
    for copy in copies:
        copy.start()
    for r, grad in enumerate(own_grads(w_conv, pre, z, channels, rows, lon, 1)):
        main[r] = (grad + total_row(r, rows, channels, cot, member)).astype(BF16)
    for copy in copies:
        copy.wait()


def forward(member, rounded, low, high, turned, column, w_conv, w_out, cot, land):
    _, rows, channels, lon = rounded.shape
    taps, width = w_conv.shape
    cols, more = rows * lon, (rows + 2) * lon
    operands = [rounded, low, high, turned, column, w_conv, w_out, cot, land]
    specs = [full_block(x.shape) for x in operands]
    main = (rows, channels, lon)
    hbm = pl.BlockSpec(memory_space=pltpu.HBM)
    return pl.pallas_call(
        functools.partial(forward_body, member),
        grid=(1,),
        in_specs=specs,
        out_specs=[full_block(main), hbm, hbm],
        out_shape=[jax.ShapeDtypeStruct(main, BF16), pltpu.HBM((width, cols), BF16), pltpu.HBM((width, cols), F32)],
        scratch_shapes=[
            pltpu.VMEM((3 * channels, (rows + 4) * lon), BF16),
            pltpu.VMEM((width, more), BF16),
            pltpu.VMEM((width, more), F32),
            pltpu.VMEM((channels, more), BF16),
            pltpu.VMEM((width, more), BF16),
            pltpu.VMEM((taps, more), F32),
            pltpu.SemaphoreType.DMA((2,)),
        ],
        compiler_params=PARAMS,
    )(*operands)


def phase_bits(parts, core):
    bits = list(range(parts.bit_length() - 1))
    if len(bits) > 2 and core == 1:
        bits[1], bits[2] = bits[2], bits[1]
    return bits


def place_of(relative, core, parts):
    even, odd = phase_bits(parts, 0), phase_bits(parts, 1)
    depth = len(even)
    place = 0
    for i in range(1, depth):
        bit = (relative >> even[i]) & 1
        if even[i] != odd[i]:
            bit = jnp.where(core == 0, bit, (relative >> odd[i]) & 1)
        place = place + (bit << (depth - 1 - i))
    return place


def weight_body(member, first, last, parts, here_ref, *refs):
    rounded, low, high, cot, land, w_out, w_conv, main, hidden_in, slope_in = refs[:10]
    refs = refs[10:]
    if not first:
        up_in, down_in, w1_in, w2_in, acc_in = refs[:5]
        refs = refs[5:]
        for m in range(member):
            refs[0][m] = up_in[m]
            refs[1][m] = down_in[m]
    up, down, pre = refs[:3]
    if last:
        give, keep, hidden, slope, stack, masked, sems, w1, w2 = refs[3:]
    else:
        w1, w2, acc_out, hidden, slope, stack, masked, sems = refs[3:]
    _, rows, channels, lon = rounded.shape
    width = w_out.shape[0]
    cols = rows * lon
    copies = [
        pltpu.make_async_copy(hidden_in, hidden, sems.at[0]),
        pltpu.make_async_copy(slope_in, slope, sems.at[1]),
    ]
    for copy in copies:
        copy.start()
    build_stack(rounded, low, high, stack, member, 1)
    for r in range(rows):
        masked[:, r * lon : (r + 1) * lon] = masked_row(
            r, land, total_row(r, rows, channels, cot, member, main)
        )
    copies[0].wait()
    part = dot_t(hidden[...], masked[...])
    w2[...] = part if first else part + w2_in[...]
    acc = None if first else acc_in[...]
    copies[1].wait()
    for k in range(0, rows, 2):
        at = slice(k * lon, (k + 2) * lon)
        grad = dot(w_out[...], masked[:, at]) * slope[:, at]
        pre[:, at] = grad.astype(BF16)
        both = grad[:, :lon] + grad[:, lon:]
        acc = both if acc is None else acc + both
    above, below = edge_grads(w_conv, pre, channels, rows, lon)
    up[member] = above.astype(BF16)
    down[member] = below.astype(BF16)
    for rs in range(3):
        at = slice(rs * 3 * channels, (rs + 1) * 3 * channels)
        part = dot_t(stack[:, rs * lon : rs * lon + cols], pre[...])
        w1[at, :] = part if first else part + w1_in[at, :]
    if not last:
        acc_out[...] = acc
        return

    here = here_ref[0]
    core = here & 1
    line = jnp.sum(acc.T, axis=0, keepdims=True)
    deep, wide = w1.shape[0] // parts, width // parts
    folds = width // channels
    thin = wide // folds

    def fill(target, place, t):
        kind = target.dtype
        target[place, 0:deep, :] = w1[t * deep : (t + 1) * deep, :].astype(kind)
        for f in range(folds):
            target[place, deep : deep + thin, f * channels : (f + 1) * channels] = w2[
                t * wide + f * thin : t * wide + (f + 1) * thin, :
            ].astype(kind)
        shifted = line if t == 0 else pltpu.roll(line, width - t * wide, 1)
        target[place, deep + thin : deep + thin + 1, :] = shifted.astype(kind)

    for t in range(parts):
        relative = here ^ t

        @pl.when((relative & 1) == 0)
        def _():
            fill(keep, place_of(relative, core, parts), t)

        @pl.when((relative & 1) == 1)
        def _():
            fill(give, place_of(relative, 1 - core, parts), t)


def packed_rows(taps, width, channels, parts):
    used = taps // parts + width // parts // (width // channels) + 1
    return -(-used // 8) * 8


def weight(member, here, parts, rounded, low, high, cot, land, w_out, w_conv, main, kept, before):
    members, rows, channels, lon = rounded.shape
    taps, width = w_conv.shape
    cols = rows * lon
    first, last = member == 0, member + 1 == members

    def full(shape):
        return pl.BlockSpec(tuple(shape), lambda i, _: (0,) * len(shape))

    operands = [rounded, low, high, cot, land, w_out, w_conv, main]
    specs = [full(x.shape) for x in operands]
    operands += [pltpu.with_memory_space_constraint(x, pltpu.HBM) for x in kept]
    specs += [pl.BlockSpec(memory_space=pltpu.HBM) for _ in kept]
    operands += before
    specs += [full(x.shape) for x in before]
    edge = (member + 1, channels, lon)
    sums = [((taps, width), F32), ((width, channels), F32)]
    shapes = [(edge, BF16), (edge, BF16), ((width, cols), BF16)]
    if last:
        chunk = (parts // 2, packed_rows(taps, width, channels, parts), width)
        shapes += [(chunk, BF16), (chunk, F32)]
    else:
        shapes += sums + [((width, lon), F32)]
    return pl.pallas_call(
        functools.partial(weight_body, member, first, last, parts),
        grid_spec=pltpu.PrefetchScalarGridSpec(
            num_scalar_prefetch=1,
            grid=(1,),
            in_specs=specs,
            out_specs=[full(s) for s, _ in shapes],
            scratch_shapes=[pltpu.VMEM(x.shape, x.dtype) for x in kept]
            + [
                pltpu.VMEM((3 * channels, (rows + 2) * lon), BF16),
                pltpu.VMEM((channels, cols), BF16),
                pltpu.SemaphoreType.DMA((2,)),
            ]
            + ([pltpu.VMEM(s, d) for s, d in sums] if last else []),
        ),
        out_shape=[jax.ShapeDtypeStruct(s, d) for s, d in shapes],
        compiler_params=PARAMS,
    )(here, *operands)


def state_body(members, w_conv, cot, beside_low, beside_high, *refs):
    pres, mains = refs[:members], refs[members : 2 * members]
    out, z, local, sems = refs[2 * members :]
    rows, channels, lon = mains[0].shape
    copies = [pltpu.make_async_copy(local.at[m], out.at[m], sems.at[m]) for m in range(members)]
    for m in range(members):
        for r, grad in enumerate(own_grads(w_conv, pres[m], z.at[m % 2], channels, rows, lon, 0)):
            total = grad + total_row(r, rows, channels, cot, m, mains[m])
            if r == 0:
                total = total + beside_low[m].astype(F32)
            if r == rows - 1:
                total = total + beside_high[m].astype(F32)
            local[m, pl.ds(r, channels, stride=rows), :] = total
        copies[m].start()
    for copy in copies:
        copy.wait()


def state_grad(w_conv, cot, beside_low, beside_high, pres, mains):
    taps = w_conv.shape[0]
    operands = [w_conv, cot, beside_low, beside_high, *pres, *mains]
    return pl.pallas_call(
        functools.partial(state_body, len(pres)),
        grid=(1,),
        in_specs=[full_block(x.shape) for x in operands],
        out_specs=pl.BlockSpec(memory_space=pltpu.HBM),
        out_shape=pltpu.HBM(cot.shape, F32),
        scratch_shapes=[
            pltpu.VMEM((2, taps, pres[0].shape[1]), F32),
            pltpu.VMEM(cot.shape, F32),
            pltpu.SemaphoreType.DMA((len(pres),)),
        ],
        compiler_params=PARAMS,
        name="state",
    )(*operands)


def finish_body(scale, own, taken, w1, w2, b1):
    deep = w1.shape[0]
    wide, channels = w2.shape
    folds = own.shape[2] // channels
    thin = wide // folds
    total = (own[0] + taken[0].astype(F32)) * scale
    w1[...] = total[:deep]
    for f in range(folds):
        w2[f * thin : (f + 1) * thin, :] = total[deep : deep + thin, f * channels : (f + 1) * channels]
    b1[...] = total[deep + thin : deep + thin + 1, :wide]


def finish(scale, own, taken, deep, wide, channels):
    return pl.pallas_call(
        functools.partial(finish_body, scale),
        out_shape=[
            jax.ShapeDtypeStruct((deep, own.shape[2]), F32),
            jax.ShapeDtypeStruct((wide, channels), F32),
            jax.ShapeDtypeStruct((1, wide), F32),
        ],
        compiler_params=PARAMS,
        name="finish",
    )(own, taken)


def shards(states, cotangents, w_conv, b_conv, w_out, forcing, land, dates):
    section = lax.axis_index("lead").astype(jnp.int32)
    here = lax.axis_index("tile").astype(jnp.int32)
    leads = lax.axis_size("lead")
    tiles = lax.axis_size("tile")
    _, members, channels, rows, lon = states.shape
    taps, width = w_conv.shape
    own = states.reshape(members, channels * rows, lon)
    cot = cotangents.reshape(members, channels * rows, lon)
    rounded, top, bottom = prep(dates, section[None], forcing, own, cot, land)
    ahead = [(t, t + 1) for t in range(tiles - 1)]
    behind = [(t + 1, t) for t in range(tiles - 1)]
    low = lax.ppermute(bottom, "tile", ahead)
    high = lax.ppermute(top, "tile", behind)
    turned, column = turn(w_conv, b_conv[None, :], lon)

    steps = [(s, s - 1) for s in range(1, leads)]
    kept = []
    mains = []
    for m in range(members):
        main, hidden, slope = forward(m, rounded, low, high, turned, column, w_conv, w_out, cot, land)
        kept.append((hidden, slope))
        mains.append(lax.ppermute(main, "lead", steps))
    before = []
    pres = []
    for m in range(members):
        up, down, pre, *sums = weight(
            m, here[None], tiles, rounded, low, high, cot, land, w_out, w_conv, mains[m], kept[m], before
        )
        before = [up, down, *sums]
        pres.append(pre)
    give, keep = sums
    assert tiles >= 8

    def exchanged(value, step):
        bits = (phase_bits(tiles, 0)[step], phase_bits(tiles, 1)[step])
        return lax.ppermute(value, "tile", [(t, t ^ (1 << bits[t & 1])) for t in range(tiles)])

    total = keep + exchanged(give, 0).astype(F32)
    for step in range(1, tiles.bit_length() - 1):
        half = total.shape[0] // 2
        send = total[half:].astype(BF16)
        if step == 1:
            send, up, down = lax.optimization_barrier((send, up, down))
            beside_low = lax.ppermute(down, "tile", ahead)
            beside_high = lax.ppermute(up, "tile", behind)
        if step == STATE_STEP:
            send, *pres = lax.optimization_barrier((send, *pres))
            body = state_grad(w_conv, cot, beside_low, beside_high, pres, mains)
        taken = exchanged(send, step)
        if step == STATE_STEP:
            taken, body = lax.optimization_barrier((taken, body))
        total = total[:half] + taken.astype(F32)
    grads = body.reshape(states.shape)
    taken = lax.ppermute(total.astype(BF16), "lead", [(s, leads - 1 - s) for s in range(leads)])
    scale = 1.0 / math.sqrt(leads * members * rows * tiles * lon)
    w1, w2, b1 = finish(scale, total, taken, taps // tiles, width // tiles, channels)
    return grads, w1, w2, b1[0]


def solution(mesh):
    assert mesh.shape["lead"] == 2
    placed = (
        P("lead", None, None, "tile", None),
        P("lead", None, None, "tile", None),
        P(),
        P(),
        P(),
        P(),
        P("tile", None),
        P(),
    )
    return jax.shard_map(
        shards,
        mesh=mesh,
        in_specs=placed,
        out_specs=(
            P("lead", None, None, "tile", None),
            P("tile", None),
            P("tile", None),
            P("tile"),
        ),
        check_vma=False,
    )
```

```python
import functools
import math

import jax
import jax.numpy as jnp
from jax import lax
from jax.experimental import pallas as pl
from jax.experimental.pallas import tpu as pltpu
from jax.sharding import PartitionSpec as P


TANH_SCALE = 0.7978845608028654
CUBIC_TERM = 0.044715
BF16 = jnp.bfloat16
F32 = jnp.float32
STATE_STEP = 3
PARAMS = pltpu.CompilerParams(vmem_limit_bytes=32 * 1024 * 1024)


def dot(left, right):
    return jnp.dot(left, right, preferred_element_type=F32)


def dot_t(left, right):
    return lax.dot_general(left, right, (((1,), (1,)), ((), ())), preferred_element_type=F32)


def gelu_pair(v):
    square = v * v
    half = 0.5 + 0.5 * jnp.tanh(v * (TANH_SCALE + (TANH_SCALE * CUBIC_TERM) * square))
    value = v * half
    slope = half + value * (1.0 - half) * (2.0 * TANH_SCALE + (6.0 * TANH_SCALE * CUBIC_TERM) * square)
    return value, slope


def full_block(shape):
    return pl.BlockSpec(tuple(shape), lambda i: (0,) * len(shape))


def prep_body(rows, dates, section, forcing, states, cot, land, rounded, top, bottom):
    m = pl.program_id(0)
    days, channels = forcing.shape
    lon = states.shape[2]
    day = (dates[m] + section[0]) % days
    line = forcing[pl.ds(day, 1), :]
    shift = jnp.broadcast_to(line, (lon, channels)).T
    for r in range(rows):
        value = (states[0, pl.ds(r, channels, stride=rows), :] + shift).astype(BF16)
        rounded[0, r] = value
        if r < 2:
            top[0, r] = value
        if r >= rows - 2:
            bottom[0, r - (rows - 2)] = value
    top[0, 2] = masked_row(0, land, total_row(0, rows, channels, cot, 0))
    bottom[0, 2] = masked_row(rows - 1, land, total_row(rows - 1, rows, channels, cot, 0))


def prep(dates, section, forcing, states, cot, land):
    members, flat, lon = states.shape
    rows = land.shape[0]
    channels = flat // rows
    smem = pl.BlockSpec(memory_space=pltpu.SMEM)
    own = pl.BlockSpec((1, flat, lon), lambda m: (m, 0, 0))
    halo = pl.BlockSpec((1, 3, channels, lon), lambda m: (m, 0, 0, 0))
    return pl.pallas_call(
        functools.partial(prep_body, rows),
        grid=(members,),
        in_specs=[smem, smem, full_block(forcing.shape), own, own, full_block(land.shape)],
        out_specs=[pl.BlockSpec((1, rows, channels, lon), lambda m: (m, 0, 0, 0)), halo, halo],
        out_shape=[
            jax.ShapeDtypeStruct((members, rows, channels, lon), BF16),
            jax.ShapeDtypeStruct((members, 3, channels, lon), BF16),
            jax.ShapeDtypeStruct((members, 3, channels, lon), BF16),
        ],
        name="prep",
    )(dates, section, forcing, states, cot, land)


def turn_body(w_conv, b_conv, turned, column):
    turned[...] = w_conv[...].T
    column[...] = jnp.broadcast_to(b_conv[...], (column.shape[1], column.shape[0])).T


def turn(w_conv, b_conv, lanes):
    taps, hidden = w_conv.shape
    return pl.pallas_call(
        turn_body,
        out_shape=[
            jax.ShapeDtypeStruct((hidden, taps), BF16),
            jax.ShapeDtypeStruct((hidden, lanes), F32),
        ],
        compiler_params=PARAMS,
        name="turn",
    )(w_conv, b_conv)


def edge_grads(w_conv, pre, channels, rows, lon):
    out = []
    for rs, source in ((0, 0), (2, rows - 1)):
        block = w_conv[rs * 3 * channels : (rs + 1) * 3 * channels, :]
        part = dot(block, pre[:, source * lon : (source + 1) * lon])
        out.append(
            part[channels : 2 * channels]
            + pltpu.roll(part[:channels], lon - 1, 1)
            + pltpu.roll(part[2 * channels :], 1, 1)
        )
    return out


def row_sums(z, place, channels, rows, lon):
    for i in range(rows):
        per_step = []
        for cs in range(3):
            total = None
            for rs in range(3):
                source = i - (rs - 1)
                if source in place:
                    tap = 3 * rs + cs
                    at = place[source] * lon
                    term = z[tap * channels : (tap + 1) * channels, at : at + lon]
                    total = term if total is None else total + term
            per_step.append(total)
        yield per_step[1] + pltpu.roll(per_step[0], lon - 1, 1) + pltpu.roll(per_step[2], 1, 1)


def total_row(r, rows, channels, cot, member, main=None):
    total = cot[member, pl.ds(r, channels, stride=rows), :]
    return total if main is None else total + main[r].astype(F32)


def masked_row(r, land, total):
    return (land[r : r + 1, :].astype(F32) * total).astype(BF16)


def state_line(q, rounded, low, high, member):
    rows = rounded.shape[1]
    if q < 0:
        return low[member, 2 + q]
    return high[member, q - rows] if q >= rows else rounded[member, q]


def build_stack(lines, stack):
    channels, lon = lines[0].shape
    for q, x in enumerate(lines):
        wide = x.astype(F32)
        at = slice(q * lon, (q + 1) * lon)
        stack[0:channels, at] = pltpu.roll(wide, 1, 1).astype(BF16)
        stack[channels : 2 * channels, at] = x
        stack[2 * channels : 3 * channels, at] = pltpu.roll(wide, lon - 1, 1).astype(BF16)


def two_rows(turned, stack, start, bias, lon):
    channels = stack.shape[0] // 3
    preact = bias
    for rs in range(3):
        preact = preact + dot(
            turned[:, rs * 3 * channels : (rs + 1) * 3 * channels],
            stack[:, (start + rs) * lon : (start + rs + 2) * lon],
        )
    return gelu_pair(preact)


def inner_body(members, rounded, turned, column, w_out, cot, land, *refs):
    pres, hidden_out, slope_out = (refs[i * members : (i + 1) * members] for i in range(3))
    stack, hidden, slope, masked, sems = refs[3 * members :]
    _, rows, channels, lon = rounded.shape
    bias = jnp.concatenate([column[...], column[...]], axis=1)
    copies = []
    for m in range(members):
        build_stack([rounded[m, q] for q in range(rows)], stack.at[m])
        for r in range(1, rows - 1):
            masked[m, :, (r - 1) * lon : r * lon] = masked_row(
                r, land, total_row(r, rows, channels, cot, m)
            )
        for k in range(0, rows - 2, 2):
            value, steep = two_rows(turned, stack.at[m], k, bias, lon)
            cols = slice(k * lon, (k + 2) * lon)
            hidden[m, :, cols] = value.astype(BF16)
            slope[m, :, cols] = steep
            pres[m][:, cols] = (dot(w_out[...], masked[m, :, cols]) * steep).astype(BF16)
        copies.append(pltpu.make_async_copy(hidden.at[m], hidden_out[m], sems.at[m, 0]))
        copies.append(pltpu.make_async_copy(slope.at[m], slope_out[m], sems.at[m, 1]))
        copies[-2].start()
        copies[-1].start()
    for copy in copies:
        copy.wait()


def inner(rounded, turned, column, w_out, cot, land):
    members, rows, channels, lon = rounded.shape
    assert rows % 2 == 0 and rows >= 4
    width = turned.shape[0]
    cols = (rows - 2) * lon
    operands = [rounded, turned, column, w_out, cot, land]
    hbm = pl.BlockSpec(memory_space=pltpu.HBM)
    outs = pl.pallas_call(
        functools.partial(inner_body, members),
        grid=(1,),
        in_specs=[full_block(x.shape) for x in operands],
        out_specs=[full_block((width, cols))] * members + [hbm] * (2 * members),
        out_shape=[jax.ShapeDtypeStruct((width, cols), BF16)] * members
        + [pltpu.HBM((width, cols), BF16)] * members
        + [pltpu.HBM((width, cols), F32)] * members,
        scratch_shapes=[
            pltpu.VMEM((members, 3 * channels, rows * lon), BF16),
            pltpu.VMEM((members, width, cols), BF16),
            pltpu.VMEM((members, width, cols), F32),
            pltpu.VMEM((members, channels, cols), BF16),
            pltpu.SemaphoreType.DMA((members, 2)),
        ],
        compiler_params=PARAMS,
        name="inner",
    )(*operands)
    return outs[:members], outs[members : 2 * members], outs[2 * members :]


def forward_body(
    member, rounded, low, high, turned, column, w_conv, w_out, cot, land, pre_in,
    main, hidden_out, slope_out, stack, hidden, slope, masked, pre, z, sems,
):
    _, rows, channels, lon = rounded.shape
    taps = 9 * channels
    lines = [*range(-2, 2), *range(rows - 2, rows + 2)]
    build_stack([state_line(q, rounded, low, high, member) for q in lines], stack)
    masked[:, 0:lon] = low[member, 2]
    for i, r in ((1, 0), (2, rows - 1)):
        masked[:, i * lon : (i + 1) * lon] = masked_row(
            r, land, total_row(r, rows, channels, cot, member)
        )
    masked[:, 3 * lon :] = high[member, 2]
    bias = jnp.concatenate([column[...], column[...]], axis=1)
    for side in range(2):
        value, steep = two_rows(turned, stack, 4 * side, bias, lon)
        cols = slice(2 * side * lon, (2 * side + 2) * lon)
        hidden[:, cols] = value.astype(BF16)
        slope[:, cols] = steep
        pre[:, cols] = (dot(w_out[...], masked[:, cols]) * steep).astype(BF16)
    middle = slice(lon, 3 * lon)
    copies = [
        pltpu.make_async_copy(hidden.at[:, middle], hidden_out, sems.at[0]),
        pltpu.make_async_copy(slope.at[:, middle], slope_out, sems.at[1]),
    ]
    for copy in copies:
        copy.start()
    place = {-1: 0, 0: 1, rows - 1: 2, rows: 3}
    for k in range(0, rows - 2, 2):
        place[k + 1], place[k + 2] = 4 + k, 5 + k
        z[0:taps, (4 + k) * lon : (6 + k) * lon] = dot(w_conv[...], pre_in[:, k * lon : (k + 2) * lon])
    z[0:taps, middle] = dot(w_conv[...], pre[:, middle])
    for at, rs in ((0, 2), (3, 0)):
        cols = slice(at * lon, (at + 1) * lon)
        block = slice(rs * 3 * channels, (rs + 1) * 3 * channels)
        z[block, cols] = dot(w_conv[block, :], pre[:, cols])
    for r, grad in enumerate(row_sums(z, place, channels, rows, lon)):
        main[r] = (grad + total_row(r, rows, channels, cot, member)).astype(BF16)
    for copy in copies:
        copy.wait()


def forward(member, rounded, low, high, turned, column, w_conv, w_out, cot, land, pre_in):
    _, rows, channels, lon = rounded.shape
    taps, width = w_conv.shape
    operands = [rounded, low, high, turned, column, w_conv, w_out, cot, land, pre_in]
    main = (rows, channels, lon)
    hbm = pl.BlockSpec(memory_space=pltpu.HBM)
    kept = (width, 2 * lon)
    return pl.pallas_call(
        functools.partial(forward_body, member),
        grid=(1,),
        in_specs=[full_block(x.shape) for x in operands],
        out_specs=[full_block(main), hbm, hbm],
        out_shape=[jax.ShapeDtypeStruct(main, BF16), pltpu.HBM(kept, BF16), pltpu.HBM(kept, F32)],
        scratch_shapes=[
            pltpu.VMEM((3 * channels, 8 * lon), BF16),
            pltpu.VMEM((width, 4 * lon), BF16),
            pltpu.VMEM((width, 4 * lon), F32),
            pltpu.VMEM((channels, 4 * lon), BF16),
            pltpu.VMEM((width, 4 * lon), BF16),
            pltpu.VMEM((taps, (rows + 2) * lon), F32),
            pltpu.SemaphoreType.DMA((2,)),
        ],
        compiler_params=PARAMS,
    )(*operands)


def phase_bits(parts, core):
    bits = list(range(parts.bit_length() - 1))
    if len(bits) > 2 and core == 1:
        bits[1], bits[2] = bits[2], bits[1]
    return bits


def place_of(relative, core, parts):
    even, odd = phase_bits(parts, 0), phase_bits(parts, 1)
    depth = len(even)
    place = 0
    for i in range(1, depth):
        bit = (relative >> even[i]) & 1
        if even[i] != odd[i]:
            bit = jnp.where(core == 0, bit, (relative >> odd[i]) & 1)
        place = place + (bit << (depth - 1 - i))
    return place


def weight_body(member, first, last, parts, here_ref, *refs):
    rounded, low, high, cot, land, w_out, w_conv, main = refs[:8]
    held = refs[8:12]
    refs = refs[12:]
    if not first:
        up_in, down_in, w1_in, w2_in, acc_in = refs[:5]
        refs = refs[5:]
        for m in range(member):
            refs[0][m] = up_in[m]
            refs[1][m] = down_in[m]
    up, down, pre = refs[:3]
    if last:
        give, keep, hidden, slope, stack, masked, sems, w1, w2 = refs[3:]
    else:
        w1, w2, acc_out, hidden, slope, stack, masked, sems = refs[3:]
    _, rows, channels, lon = rounded.shape
    width = w_out.shape[0]
    cols = rows * lon
    parts_of = [slice(lon, cols - lon), slice(0, lon), slice(cols - lon, cols)]
    copies = []
    for i, target in enumerate((hidden, slope)):
        middle, outer = held[2 * i : 2 * i + 2]
        sources = [middle, outer.at[:, 0:lon], outer.at[:, lon : 2 * lon]]
        copies.append(
            [
                pltpu.make_async_copy(source, target.at[:, at], sems.at[i, j])
                for j, (source, at) in enumerate(zip(sources, parts_of))
            ]
        )
        for copy in copies[-1]:
            copy.start()
    build_stack([state_line(q, rounded, low, high, member) for q in range(-1, rows + 1)], stack)
    for r in range(rows):
        masked[:, r * lon : (r + 1) * lon] = masked_row(
            r, land, total_row(r, rows, channels, cot, member, main)
        )
    for copy in copies[0]:
        copy.wait()
    part = dot_t(hidden[...], masked[...])
    w2[...] = part if first else part + w2_in[...]
    acc = None if first else acc_in[...]
    for copy in copies[1]:
        copy.wait()
    for k in range(0, rows, 2):
        at = slice(k * lon, (k + 2) * lon)
        grad = dot(w_out[...], masked[:, at]) * slope[:, at]
        pre[:, at] = grad.astype(BF16)
        both = grad[:, :lon] + grad[:, lon:]
        acc = both if acc is None else acc + both
    above, below = edge_grads(w_conv, pre, channels, rows, lon)
    up[member] = above.astype(BF16)
    down[member] = below.astype(BF16)
    for rs in range(3):
        at = slice(rs * 3 * channels, (rs + 1) * 3 * channels)
        part = dot_t(stack[:, rs * lon : rs * lon + cols], pre[...])
        w1[at, :] = part if first else part + w1_in[at, :]
    if not last:
        acc_out[...] = acc
        return

    here = here_ref[0]
    core = here & 1
    line = jnp.sum(acc.T, axis=0, keepdims=True)
    deep, wide = w1.shape[0] // parts, width // parts
    folds = width // channels
    thin = wide // folds

    def fill(target, place, t):
        kind = target.dtype
        target[place, 0:deep, :] = w1[t * deep : (t + 1) * deep, :].astype(kind)
        for f in range(folds):
            target[place, deep : deep + thin, f * channels : (f + 1) * channels] = w2[
                t * wide + f * thin : t * wide + (f + 1) * thin, :
            ].astype(kind)
        shifted = line if t == 0 else pltpu.roll(line, width - t * wide, 1)
        target[place, deep + thin : deep + thin + 1, :] = shifted.astype(kind)

    for t in range(parts):
        relative = here ^ t

        @pl.when((relative & 1) == 0)
        def _():
            fill(keep, place_of(relative, core, parts), t)

        @pl.when((relative & 1) == 1)
        def _():
            fill(give, place_of(relative, 1 - core, parts), t)


def packed_rows(taps, width, channels, parts):
    used = taps // parts + width // parts // (width // channels) + 1
    return -(-used // 8) * 8


def weight(member, here, parts, rounded, low, high, cot, land, w_out, w_conv, main, kept, before):
    members, rows, channels, lon = rounded.shape
    taps, width = w_conv.shape
    cols = rows * lon
    first, last = member == 0, member + 1 == members

    def full(shape):
        return pl.BlockSpec(tuple(shape), lambda i, _: (0,) * len(shape))

    operands = [rounded, low, high, cot, land, w_out, w_conv, main]
    specs = [full(x.shape) for x in operands]
    operands += [pltpu.with_memory_space_constraint(x, pltpu.HBM) for x in kept]
    specs += [pl.BlockSpec(memory_space=pltpu.HBM) for _ in kept]
    operands += before
    specs += [full(x.shape) for x in before]
    edge = (member + 1, channels, lon)
    sums = [((taps, width), F32), ((width, channels), F32)]
    shapes = [(edge, BF16), (edge, BF16), ((width, cols), BF16)]
    if last:
        chunk = (parts // 2, packed_rows(taps, width, channels, parts), width)
        shapes += [(chunk, BF16), (chunk, F32)]
    else:
        shapes += sums + [((width, lon), F32)]
    return pl.pallas_call(
        functools.partial(weight_body, member, first, last, parts),
        grid_spec=pltpu.PrefetchScalarGridSpec(
            num_scalar_prefetch=1,
            grid=(1,),
            in_specs=specs,
            out_specs=[full(s) for s, _ in shapes],
            scratch_shapes=[pltpu.VMEM((width, cols), BF16), pltpu.VMEM((width, cols), F32)]
            + [
                pltpu.VMEM((3 * channels, (rows + 2) * lon), BF16),
                pltpu.VMEM((channels, cols), BF16),
                pltpu.SemaphoreType.DMA((2, 3)),
            ]
            + ([pltpu.VMEM(s, d) for s, d in sums] if last else []),
        ),
        out_shape=[jax.ShapeDtypeStruct(s, d) for s, d in shapes],
        compiler_params=PARAMS,
    )(here, *operands)


def state_body(members, w_conv, cot, beside_low, beside_high, *refs):
    pres, mains = refs[:members], refs[members : 2 * members]
    out, z, local, sems = refs[2 * members :]
    rows, channels, lon = mains[0].shape
    copies = [pltpu.make_async_copy(local.at[m], out.at[m], sems.at[m]) for m in range(members)]
    for m in range(members):
        for k in range(0, rows, 2):
            at = slice(k * lon, (k + 2) * lon)
            z[m % 2, :, at] = dot(w_conv[...], pres[m][:, at])
        place = {r: r for r in range(rows)}
        for r, grad in enumerate(row_sums(z.at[m % 2], place, channels, rows, lon)):
            total = grad + total_row(r, rows, channels, cot, m, mains[m])
            if r == 0:
                total = total + beside_low[m].astype(F32)
            if r == rows - 1:
                total = total + beside_high[m].astype(F32)
            local[m, pl.ds(r, channels, stride=rows), :] = total
        copies[m].start()
    for copy in copies:
        copy.wait()


def state_grad(w_conv, cot, beside_low, beside_high, pres, mains):
    taps = w_conv.shape[0]
    operands = [w_conv, cot, beside_low, beside_high, *pres, *mains]
    return pl.pallas_call(
        functools.partial(state_body, len(pres)),
        grid=(1,),
        in_specs=[full_block(x.shape) for x in operands],
        out_specs=pl.BlockSpec(memory_space=pltpu.HBM),
        out_shape=pltpu.HBM(cot.shape, F32),
        scratch_shapes=[
            pltpu.VMEM((2, taps, pres[0].shape[1]), F32),
            pltpu.VMEM(cot.shape, F32),
            pltpu.SemaphoreType.DMA((len(pres),)),
        ],
        compiler_params=PARAMS,
        name="state",
    )(*operands)


def finish_body(scale, own, taken, w1, w2, b1):
    deep = w1.shape[0]
    wide, channels = w2.shape
    folds = own.shape[2] // channels
    thin = wide // folds
    total = (own[0] + taken[0].astype(F32)) * scale
    w1[...] = total[:deep]
    for f in range(folds):
        w2[f * thin : (f + 1) * thin, :] = total[deep : deep + thin, f * channels : (f + 1) * channels]
    b1[...] = total[deep + thin : deep + thin + 1, :wide]


def finish(scale, own, taken, deep, wide, channels):
    return pl.pallas_call(
        functools.partial(finish_body, scale),
        out_shape=[
            jax.ShapeDtypeStruct((deep, own.shape[2]), F32),
            jax.ShapeDtypeStruct((wide, channels), F32),
            jax.ShapeDtypeStruct((1, wide), F32),
        ],
        compiler_params=PARAMS,
        name="finish",
    )(own, taken)


def shards(states, cotangents, w_conv, b_conv, w_out, forcing, land, dates):
    section = lax.axis_index("lead").astype(jnp.int32)
    here = lax.axis_index("tile").astype(jnp.int32)
    leads = lax.axis_size("lead")
    tiles = lax.axis_size("tile")
    _, members, channels, rows, lon = states.shape
    taps, width = w_conv.shape
    own = states.reshape(members, channels * rows, lon)
    cot = cotangents.reshape(members, channels * rows, lon)
    rounded, top, bottom = prep(dates, section[None], forcing, own, cot, land)
    ahead = [(t, t + 1) for t in range(tiles - 1)]
    behind = [(t + 1, t) for t in range(tiles - 1)]
    low = lax.ppermute(bottom, "tile", ahead)
    high = lax.ppermute(top, "tile", behind)
    turned, column = turn(w_conv, b_conv[None, :], lon)
    inner_pres, inner_hidden, inner_slope = inner(rounded, turned, column, w_out, cot, land)

    steps = [(s, s - 1) for s in range(1, leads)]
    kept = []
    mains = []
    for m in range(members):
        main, hidden, slope = forward(m, rounded, low, high, turned, column, w_conv, w_out, cot, land, inner_pres[m])
        kept.append((inner_hidden[m], hidden, inner_slope[m], slope))
        mains.append(lax.ppermute(main, "lead", steps))
    before = []
    pres = []
    for m in range(members):
        up, down, pre, *sums = weight(
            m, here[None], tiles, rounded, low, high, cot, land, w_out, w_conv, mains[m], kept[m], before
        )
        before = [up, down, *sums]
        pres.append(pre)
    give, keep = sums
    assert tiles >= 8

    def exchanged(value, step):
        bits = (phase_bits(tiles, 0)[step], phase_bits(tiles, 1)[step])
        return lax.ppermute(value, "tile", [(t, t ^ (1 << bits[t & 1])) for t in range(tiles)])

    total = keep + exchanged(give, 0).astype(F32)
    for step in range(1, tiles.bit_length() - 1):
        half = total.shape[0] // 2
        send = total[half:].astype(BF16)
        if step == 1:
            send, up, down = lax.optimization_barrier((send, up, down))
            beside_low = lax.ppermute(down, "tile", ahead)
            beside_high = lax.ppermute(up, "tile", behind)
        if step == STATE_STEP:
            send, *pres = lax.optimization_barrier((send, *pres))
            body = state_grad(w_conv, cot, beside_low, beside_high, pres, mains)
        taken = exchanged(send, step)
        if step == STATE_STEP:
            taken, body = lax.optimization_barrier((taken, body))
        total = total[:half] + taken.astype(F32)
    grads = body.reshape(states.shape)
    taken = lax.ppermute(total.astype(BF16), "lead", [(s, leads - 1 - s) for s in range(leads)])
    scale = 1.0 / math.sqrt(leads * members * rows * tiles * lon)
    w1, w2, b1 = finish(scale, total, taken, taps // tiles, width // tiles, channels)
    return grads, w1, w2, b1[0]


def solution(mesh):
    assert mesh.shape["lead"] == 2
    placed = (
        P("lead", None, None, "tile", None),
        P("lead", None, None, "tile", None),
        P(),
        P(),
        P(),
        P(),
        P("tile", None),
        P(),
    )
    return jax.shard_map(
        shards,
        mesh=mesh,
        in_specs=placed,
        out_specs=(
            P("lead", None, None, "tile", None),
            P("tile", None),
            P("tile", None),
            P("tile"),
        ),
        check_vma=False,
    )
```
